256 devices in a mesh: ctx: 32 (over z_lo, x, core), ch: 8 (over z_hi, y).
Axes of the slice: x: 4, y: 4, z: 8 (z_hi: 2, z_lo: 4; z = z_hi * 4 + z_lo), core: 2. Of those that a mesh axis runs over, the one named last changes fastest.
Arguments:
- q_stream: bfloat16 [4096, 4096], P('ch', 'ctx'), may hold values from -6 to 6
- k_stream: bfloat16 [4096, 4096], P('ch', 'ctx'), may hold values from -6 to 6
- x_stream: bfloat16 [4096, 4096], P('ch', 'ctx'), may hold values from -6 to 6
- short_taps: float32 [3, 3, 4096], P(None, None, 'ch'), may hold values from -3 to 3
- skip_gain: float32 [4096], P('ch'), may hold values from -4 to 4
- filter_taps: bfloat16 [256, 4096], P('ch', 'ctx'), may hold values from -0.375 to 0.375
Outputs:
- mixed: bfloat16 [4096, 4096], P('ch', 'ctx')
The draws below stay inside these ranges and needn't reach their ends.
All inputs are finite; a program needn't handle non-finite values.
Results may differ from the reference program's by a relative error of at most 0.0049.
Values may be sent and summed in bfloat16 or wider, within the bound.
No kernel may reach another device: no remote copies, remote signals or barrier semaphores. Data moves between devices by JAX's collectives and lax.ppermute only.
A program may use at most 64 MiB of HBM per device.

```python
import jax
import jax.numpy as jnp
from jax import lax

D = 4096
GROUPS = 256
SHORT = 3
STRETCH = 128
NCHUNK = 32
SEQ = 4096


def steps_of(own_key, shape, pieces, smallest, largest):
    def one(axis_at, shards_of):
        draws = jax.random.uniform(jax.random.fold_in(jax.random.fold_in(own_key, 6), axis_at), (shards_of,), jnp.float32, smallest / len(pieces), largest / len(pieces))
        return jnp.repeat(jnp.exp(draws), shape[axis_at] // shards_of).reshape((-1,) + (1,) * (len(shape) - axis_at - 1))

    level = one(*pieces[0])
    for cut in pieces[1:]:
        level = level * one(*cut)
    return level


def centred(stream_key, extent, scale, limit, pieces=(), held_as=jnp.bfloat16):
    drawn = scale * jax.random.normal(stream_key, extent, jnp.float32)
    if pieces:
        drawn = drawn * steps_of(stream_key, extent, pieces, -0.22, 0.18)
    return jnp.clip(drawn, -limit, limit).astype(held_as)


def setup_inputs(seed: int = 0) -> dict:
    streams_of = jax.random.split(jax.random.key(seed), 7)
    return {
        "q_stream": centred(streams_of[0], (D, SEQ), 1.0, 6.0, ((0, 8), (1, 32))),
        "k_stream": centred(streams_of[1], (D, SEQ), 1.0, 6.0, ((0, 8), (1, 32))),
        "x_stream": centred(streams_of[2], (D, SEQ), 1.0, 6.0, ((0, 8), (1, 32))),
        "short_taps": centred(streams_of[3], (3, SHORT, D), 0.6, 3.0, ((2, 8),), jnp.float32),
        "skip_gain": centred(streams_of[4], (D,), 1.0, 4.0, ((0, 8),), jnp.float32),
        "filter_taps": centred(streams_of[5], (GROUPS, SEQ), (2 * STRETCH) ** -0.5, 0.375, ((0, 8), (1, 32))),
    }


def short_conv(stream, before, weights):
    joined = jnp.concatenate([before, stream], axis=1).astype(jnp.float32)
    length = stream.shape[1]
    return (weights[0][:, None] * joined[:, 2:] + weights[1][:, None] * joined[:, 1:length + 1]
            + weights[2][:, None] * joined[:, 0:length])


def hankel(padded, lag_start, stretch_rows):
    group_count = padded.shape[0]
    segment = lax.dynamic_slice_in_dim(padded, (lag_start + 1).astype(jnp.int32), 2 * stretch_rows - 1, 1)
    segment = jnp.concatenate([segment, jnp.zeros((group_count, 1), padded.dtype)], axis=1)
    tiled = jnp.tile(segment, (1, stretch_rows + 1))
    skewed = tiled[:, :stretch_rows * (2 * stretch_rows + 1)].reshape(group_count, stretch_rows, 2 * stretch_rows + 1)
    return skewed[:, :, :stretch_rows]


def block_term(padded, lag, panel, group_width):
    group_count = padded.shape[0]
    stretch_rows = panel.shape[1]
    matrix = hankel(padded, lag * stretch_rows, stretch_rows)
    flipped = panel.reshape(group_count, group_width, stretch_rows)[:, :, ::-1]
    result = jnp.einsum('gtc,gwc->gwt', matrix.astype(jnp.float32), flipped.astype(jnp.float32))
    return result.reshape(group_count * group_width, stretch_rows)


def reference(q_stream, k_stream, x_stream, short_taps, skip_gain, filter_taps):
    before = jnp.zeros((D, 2), q_stream.dtype)
    q_short = short_conv(q_stream, before, short_taps[0])
    k_short = short_conv(k_stream, before, short_taps[1])
    x_short = short_conv(x_stream, before, short_taps[2])
    gated = (k_short * x_short).astype(jnp.bfloat16)
    padded = jnp.concatenate([jnp.zeros((GROUPS, STRETCH), filter_taps.dtype), filter_taps], axis=1)
    group_width = D // GROUPS

    def reader_block(reader):
        def add_source(source, total):
            panel = lax.dynamic_slice_in_dim(gated, (source * STRETCH).astype(jnp.int32), STRETCH, 1)
            return total + block_term(padded, reader - source, panel, group_width)

        return lax.fori_loop(jnp.int32(0), (reader + 1).astype(jnp.int32), add_source,
                             jnp.zeros((D, STRETCH), jnp.float32))

    parts = lax.map(reader_block, jnp.arange(NCHUNK, dtype=jnp.int32))
    filtered = jnp.transpose(parts, (1, 0, 2)).reshape(D, NCHUNK * STRETCH)
    mixed = q_short * (filtered + skip_gain[:, None] * gated.astype(jnp.float32))
    return mixed.astype(jnp.bfloat16)
```

```python
import jax
import jax.numpy as jnp
from jax import lax
from jax.experimental import pallas as pl
from jax.experimental.pallas import tpu as pltpu
from jax.sharding import PartitionSpec as P

INTERPRET = False
LANES = 128
ROWS = 24
F32 = jnp.float32
BF16 = jnp.bfloat16


def iota(shape, dim):
    return lax.broadcasted_iota(jnp.int32, shape, dim)


def one_hot(mask):
    return jnp.where(mask, 1.0, 0.0).astype(BF16)


def dot(a, b):
    return jnp.dot(a, b, preferred_element_type=F32)


def tap_columns(taps_ref, streams):
    rows = [taps_ref[m] for m in streams]
    count = 3 * len(streams)
    rows.append(jnp.zeros((8 - count, taps_ref.shape[2]), F32))
    return jnp.concatenate(rows, axis=0).T


def pack_kernel(k_ref, x_ref, taps_ref, lags_ref, out_ref):
    channels, length = k_ref.shape
    parts = lags_ref.shape[0]
    width = channels // parts
    columns = tap_columns(taps_ref, (1, 2))
    lane = iota((channels, length), 1)

    def short(stream, first):
        one = pltpu.roll(stream, 1, 1)
        two = pltpu.roll(stream, 2, 1)
        return (
            columns[:, first : first + 1] * stream
            + columns[:, first + 1 : first + 2] * one
            + columns[:, first + 2 : first + 3] * two
        )

    k = k_ref[...]
    x = x_ref[...]
    gated = short(k.astype(F32), 0) * short(x.astype(F32), 3)
    gated = jnp.where(lane < 2, 0.0, gated).astype(BF16)
    out_ref[:, 0:width, :] = gated.reshape(parts, width, length)

    src = iota((2 * length, length), 0)
    dst = iota((2 * length, length), 1)
    source_lane = jnp.where(dst % 4 < 2, length - 2 + dst % 4, dst % 4 - 2)
    pick = ((src % length) == source_lane) & ((src >= length) == (dst % 8 >= 4))
    spread = dot(jnp.concatenate([k, x], axis=1), one_hot(pick))
    own = (lane // 8) == (iota((channels, length), 0) % width)
    spread = jnp.where(own, spread, 0.0).astype(BF16)
    tail = 8 * parts
    row = iota((tail, channels), 0)
    gather = one_hot((row % 8 == 1) & (row // 8 == iota((tail, channels), 1) // width))
    row = iota((tail, parts), 0)
    place = one_hot((row % 8 == 0) & (row // 8 == iota((tail, parts), 1)))
    rest = dot(gather, spread) + dot(place, lags_ref[...])
    out_ref[:, width : width + 8, :] = rest.astype(BF16).reshape(parts, 8, length)


def conv_kernel(got_ref, weights_ref, skip_ref, out_ref, table_ref):
    parts, _, length = got_ref.shape
    width = out_ref.shape[1]
    rows = parts * width
    tail = got_ref[:, width : width + 8, :].reshape(8 * parts, length)

    row = iota((8 * parts, 8 * parts), 0)
    col = iota((8 * parts, 8 * parts), 1)
    lags = dot(one_hot((col // 8 == row // 8) & (col % 8 == 0)), tail)
    upper = iota((length, length), 1) >= iota((length, length), 0)
    table_ref[:, 0:length] = jnp.zeros((length, length), BF16)
    before = jnp.zeros((length, length), F32)
    for b in range(parts):
        spread = jnp.concatenate([lags[8 * b : 8 * b + 8]] * (length // 8), axis=0)
        turned = pltpu.roll(spread, 0, 1, stride=1, stride_axis=0)
        table_ref[:, (b + 1) * length : (b + 2) * length] = jnp.where(upper, turned, before).astype(BF16)
        before = turned

    row = iota((parts, 8 * parts), 0)
    col = iota((parts, 8 * parts), 1)
    edge = col % 8 == 1
    own = dot(one_hot(edge & (col // 8 == row)), tail)
    last = dot(one_hot(edge & (col // 8 + 1 == row)), tail)
    lane = iota((parts, length), 1)
    joined = jnp.where(lane % 4 < 2, last, own)
    short = (
        weights_ref[0:1, :] * joined
        + weights_ref[1:2, :] * pltpu.roll(joined, 1, 1)
        + weights_ref[2:3, :] * pltpu.roll(joined, 2, 1)
    )
    first = (short * pltpu.roll(short, length - 4, 1)).astype(BF16)
    row = iota((rows, parts), 0)
    repeated = dot(one_hot(row // width == iota((rows, parts), 1)), first)
    lane = iota((rows, length), 1)
    keep = (lane // 8 == iota((rows, length), 0) % width) & (lane % 8 >= 2) & (lane % 8 < 4)
    repeated = jnp.where(keep, repeated, 0.0).astype(BF16)
    src = iota((length, length), 0)
    dst = iota((length, length), 1)
    fixed = dot(repeated, one_hot((src % 8 - 2 == dst) & (dst < 2)))
    gated = got_ref[:, 0:width, :].reshape(rows, length).astype(F32) + fixed

    pairs = parts // 2
    split = gated.reshape(pairs, 2, width, length)
    even = split[:, 0].reshape(pairs * width, length)
    odd = split[:, 1].reshape(pairs * width, length)
    panel = jnp.concatenate([even, odd], axis=1)
    skip = jnp.concatenate([skip_ref[...]] * 2, axis=1)
    skip = jnp.concatenate([skip] * pairs, axis=0)
    total = panel * skip
    panel = panel.astype(BF16)
    for b in range(pairs):
        at = 2 * b * length
        block = jnp.concatenate(
            [table_ref[:, at + length : at + 3 * length], table_ref[:, at : at + 2 * length]], axis=0
        )
        live = (pairs - b) * width
        term = dot(panel[:live], block)
        if b:
            term = jnp.concatenate([jnp.zeros((b * width, 2 * length), F32), term], axis=0)
        total = total + term
    total = total.astype(BF16)
    halves = [total[:, 0:length], total[:, length:]]
    halves = [h.reshape(pairs, 1, width, length) for h in halves]
    out_ref[...] = jnp.concatenate(halves, axis=1).reshape(parts, width, length)


def mix_kernel(back_ref, q_ref, out_ref):
    parts, width, length = back_ref.shape
    back = back_ref[...].reshape(parts * width, length).astype(F32)
    out_ref[...] = (q_ref[...] * back).astype(BF16)


def call(kernel, out_shape, scratch=()):
    return pl.pallas_call(
        kernel,
        out_shape=out_shape,
        scratch_shapes=list(scratch),
        interpret=INTERPRET,
        name=kernel.__name__,
    )


def short_conv(stream, before, weights):
    joined = jnp.concatenate([before, stream], axis=1).astype(F32)
    length = stream.shape[1]
    return (
        weights[0][:, None] * joined[:, 2:]
        + weights[1][:, None] * joined[:, 1 : length + 1]
        + weights[2][:, None] * joined[:, 0:length]
    )


def body(q_stream, k_stream, x_stream, short_taps, skip_gain, filter_taps):
    channels, length = q_stream.shape
    parts = lax.axis_size("ctx")
    width = channels // parts
    sent = call(pack_kernel, jax.ShapeDtypeStruct((parts, ROWS, length), BF16))(
        k_stream, x_stream, short_taps, filter_taps
    )
    got = lax.all_to_all(sent, "ctx", split_axis=0, concat_axis=0, tiled=True)

    pairs = [(i, i + 1) for i in range(parts - 1)]
    before = lax.ppermute(q_stream[:, -2:], "ctx", pairs)
    q_short = lax.optimization_barrier(short_conv(q_stream, before, short_taps[0]))
    first = lax.axis_index("ctx") * width
    own = lax.dynamic_slice_in_dim(short_taps[1:], first, width, 2)
    own = jnp.repeat(jnp.transpose(own, (1, 2, 0)).reshape(3, 2 * width), 4, axis=1)
    weights = jnp.concatenate([own, jnp.zeros((5, length), F32)], axis=0)
    skip = lax.dynamic_slice_in_dim(skip_gain, first, width, 0)
    skip = jnp.broadcast_to(skip[:, None], (width, length))

    parted = call(
        conv_kernel,
        jax.ShapeDtypeStruct((parts, width, length), BF16),
        [pltpu.VMEM((length, (parts + 1) * length), BF16)],
    )(got, weights, skip)
    back = lax.all_to_all(parted, "ctx", split_axis=0, concat_axis=0, tiled=True)
    return call(mix_kernel, jax.ShapeDtypeStruct((channels, length), BF16))(back, q_short)


def solution(mesh):
    return jax.shard_map(
        body,
        mesh=mesh,
        in_specs=(
            P("ch", "ctx"),
            P("ch", "ctx"),
            P("ch", "ctx"),
            P(None, None, "ch"),
            P("ch"),
            P("ch", "ctx"),
        ),
        out_specs=P("ch", "ctx"),
        check_vma=False,
    )
```

```python
import jax
import jax.numpy as jnp
from jax import lax
from jax.experimental import pallas as pl
from jax.experimental.pallas import tpu as pltpu
from jax.sharding import PartitionSpec as P

INTERPRET = False
LANES = 128
ROWS = 24
F32 = jnp.float32
BF16 = jnp.bfloat16


def iota(shape, dim):
    return lax.broadcasted_iota(jnp.int32, shape, dim)


def one_hot(mask):
    return jnp.where(mask, 1.0, 0.0).astype(BF16)


def dot(a, b):
    return jnp.dot(a, b, preferred_element_type=F32)


def tap_columns(taps_ref, streams):
    rows = [taps_ref[m] for m in streams]
    count = 3 * len(streams)
    rows.append(jnp.zeros((8 - count, taps_ref.shape[2]), F32))
    return jnp.concatenate(rows, axis=0).T


def pack_kernel(k_ref, x_ref, taps_ref, lags_ref, out_ref):
    channels, length = k_ref.shape
    parts = lags_ref.shape[0]
    width = channels // parts
    columns = tap_columns(taps_ref, (1, 2))
    lane = iota((channels, length), 1)

    def short(stream, first):
        one = pltpu.roll(stream, 1, 1)
        two = pltpu.roll(stream, 2, 1)
        return (
            columns[:, first : first + 1] * stream
            + columns[:, first + 1 : first + 2] * one
            + columns[:, first + 2 : first + 3] * two
        )

    k = k_ref[...]
    x = x_ref[...]
    gated = short(k.astype(F32), 0) * short(x.astype(F32), 3)
    gated = jnp.where(lane < 2, 0.0, gated).astype(BF16)
    out_ref[:, 0:width, :] = gated.reshape(parts, width, length)

    src = iota((2 * length, length), 0)
    dst = iota((2 * length, length), 1)
    source_lane = jnp.where(dst % 4 < 2, length - 2 + dst % 4, dst % 4 - 2)
    pick = ((src % length) == source_lane) & ((src >= length) == (dst % 8 >= 4))
    spread = dot(jnp.concatenate([k, x], axis=1), one_hot(pick))
    own = (lane // 8) == (iota((channels, length), 0) % width)
    spread = jnp.where(own, spread, 0.0).astype(BF16)
    tail = 8 * parts
    row = iota((tail, channels), 0)
    gather = one_hot((row % 8 == 1) & (row // 8 == iota((tail, channels), 1) // width))
    row = iota((tail, parts), 0)
    place = one_hot((row % 8 == 0) & (row // 8 == iota((tail, parts), 1)))
    rest = dot(gather, spread) + dot(place, lags_ref[...])
    out_ref[:, width : width + 8, :] = rest.astype(BF16).reshape(parts, 8, length)


def conv_kernel(got_ref, weights_ref, skip_ref, out_ref, table_ref):
    parts, _, length = got_ref.shape
    width = out_ref.shape[1]
    rows = parts * width
    tail = got_ref[:, width : width + 8, :].reshape(8 * parts, length)

    row = iota((8 * parts, 8 * parts), 0)
    col = iota((8 * parts, 8 * parts), 1)
    lags = dot(one_hot((col // 8 == row // 8) & (col % 8 == 0)), tail)
    upper = iota((length, length), 1) >= iota((length, length), 0)
    table_ref[:, 0:length] = jnp.zeros((length, length), BF16)
    before = jnp.zeros((length, length), F32)
    for b in range(parts):
        spread = jnp.concatenate([lags[8 * b : 8 * b + 8]] * (length // 8), axis=0)
        turned = pltpu.roll(spread, 0, 1, stride=1, stride_axis=0)
        table_ref[:, (b + 1) * length : (b + 2) * length] = jnp.where(upper, turned, before).astype(BF16)
        before = turned

    row = iota((parts, 8 * parts), 0)
    col = iota((parts, 8 * parts), 1)
    edge = col % 8 == 1
    own = dot(one_hot(edge & (col // 8 == row)), tail)
    last = dot(one_hot(edge & (col // 8 + 1 == row)), tail)
    lane = iota((parts, length), 1)
    joined = jnp.where(lane % 4 < 2, last, own)
    short = (
        weights_ref[0:1, :] * joined
        + weights_ref[1:2, :] * pltpu.roll(joined, 1, 1)
        + weights_ref[2:3, :] * pltpu.roll(joined, 2, 1)
    )
    first = (short * pltpu.roll(short, length - 4, 1)).astype(BF16)
    row = iota((rows, parts), 0)
    repeated = dot(one_hot(row // width == iota((rows, parts), 1)), first)
    lane = iota((rows, length), 1)
    keep = (lane // 8 == iota((rows, length), 0) % width) & (lane % 8 >= 2) & (lane % 8 < 4)
    repeated = jnp.where(keep, repeated, 0.0).astype(BF16)
    src = iota((length, length), 0)
    dst = iota((length, length), 1)
    fixed = dot(repeated, one_hot((src % 8 - 2 == dst) & (dst < 2)))
    gated = got_ref[:, 0:width, :].reshape(rows, length).astype(F32) + fixed

    pairs = parts // 2
    split = gated.reshape(pairs, 2, width, length)
    even = split[:, 0].reshape(pairs * width, length)
    odd = split[:, 1].reshape(pairs * width, length)
    panel = jnp.concatenate([even, odd], axis=1)
    skip = jnp.concatenate([skip_ref[...]] * 2, axis=1)
    skip = jnp.concatenate([skip] * pairs, axis=0)
    total = panel * skip
    panel = panel.astype(BF16)
    for b in range(pairs):
        at = 2 * b * length
        block = jnp.concatenate(
            [table_ref[:, at + length : at + 3 * length], table_ref[:, at : at + 2 * length]], axis=0
        )
        live = (pairs - b) * width
        term = dot(panel[:live], block)
        if b:
            term = jnp.concatenate([jnp.zeros((b * width, 2 * length), F32), term], axis=0)
        total = total + term
    total = total.astype(BF16)
    halves = [total[:, 0:length], total[:, length:]]
    halves = [h.reshape(pairs, 1, width, length) for h in halves]
    out_ref[...] = jnp.concatenate(halves, axis=1).reshape(parts, width, length)


def mix_kernel(back_ref, q_ref, out_ref):
    parts, width, length = back_ref.shape
    back = back_ref[...].reshape(parts * width, length).astype(F32)
    out_ref[...] = (q_ref[...] * back).astype(BF16)


def call(kernel, out_shape, scratch=(), near=True):
    shape, dtype = out_shape
    out = pltpu.VMEM(shape, dtype) if near and not INTERPRET else jax.ShapeDtypeStruct(shape, dtype)
    return pl.pallas_call(
        kernel,
        out_shape=out,
        scratch_shapes=list(scratch),
        interpret=INTERPRET,
        name=kernel.__name__,
    )


def near(x):
    return x if INTERPRET else pltpu.with_memory_space_constraint(x, pltpu.VMEM)


def short_conv(stream, before, weights):
    joined = jnp.concatenate([before, stream], axis=1).astype(F32)
    length = stream.shape[1]
    return (
        weights[0][:, None] * joined[:, 2:]
        + weights[1][:, None] * joined[:, 1 : length + 1]
        + weights[2][:, None] * joined[:, 0:length]
    )


def body(q_stream, k_stream, x_stream, short_taps, skip_gain, filter_taps):
    channels, length = q_stream.shape
    parts = lax.axis_size("ctx")
    width = channels // parts
    sent = call(pack_kernel, ((parts, ROWS, length), BF16))(
        k_stream, x_stream, short_taps, filter_taps
    )
    got = lax.all_to_all(sent, "ctx", split_axis=0, concat_axis=0, tiled=True)

    pairs = [(i, i + 1) for i in range(parts - 1)]
    before = lax.ppermute(q_stream[:, -2:], "ctx", pairs)
    q_short = lax.optimization_barrier(short_conv(q_stream, before, short_taps[0]))
    first = lax.axis_index("ctx") * width
    own = lax.dynamic_slice_in_dim(short_taps[1:], first, width, 2)
    own = jnp.repeat(jnp.transpose(own, (1, 2, 0)).reshape(3, 2 * width), 4, axis=1)
    weights = jnp.concatenate([own, jnp.zeros((5, length), F32)], axis=0)
    skip = lax.dynamic_slice_in_dim(skip_gain, first, width, 0)
    skip = jnp.broadcast_to(skip[:, None], (width, length))

    parted = call(
        conv_kernel,
        ((parts, width, length), BF16),
        [pltpu.VMEM((length, (parts + 1) * length), BF16)],
    )(near(got), near(weights), near(skip))
    back = lax.all_to_all(parted, "ctx", split_axis=0, concat_axis=0, tiled=True)
    return call(mix_kernel, ((channels, length), BF16), near=False)(near(back), near(q_short))


def solution(mesh):
    return jax.shard_map(
        body,
        mesh=mesh,
        in_specs=(
            P("ch", "ctx"),
            P("ch", "ctx"),
            P("ch", "ctx"),
            P(None, None, "ch"),
            P("ch"),
            P("ch", "ctx"),
        ),
        out_specs=P("ch", "ctx"),
        check_vma=False,
    )
```

```python
import jax
import jax.numpy as jnp
from jax import lax
from jax.experimental import pallas as pl
from jax.experimental.pallas import tpu as pltpu
from jax.sharding import PartitionSpec as P

INTERPRET = False
LANES = 128
ROWS = 24
def ring_order(z0, x0, c0):
    return tuple(
        ((z + z0) % 4) * 8 + ((x + x0) % 4) * 2 + (c + c0) % 2
        for x in range(4)
        for z in range(4)
        for c in range(2)
    )


ORDER_IN = ring_order(2, 2, 1)
ORDER_OUT = ORDER_IN
F32 = jnp.float32
BF16 = jnp.bfloat16


def iota(shape, dim):
    return lax.broadcasted_iota(jnp.int32, shape, dim)


def one_hot(mask):
    return jnp.where(mask, 1.0, 0.0).astype(BF16)


def places(order):
    return [order.index(i) for i in range(len(order))]


def dot(a, b):
    return jnp.dot(a, b, preferred_element_type=F32)


def dot_t(a, b):
    return lax.dot_general(a, b, (((1,), (1,)), ((), ())), preferred_element_type=F32)


def pack_kernel(k_hbm, x_hbm, taps_hbm, lags_hbm, out_hbm, k_ref, x_ref, taps_ref, lags_ref, out_ref, sems):
    channels, length = k_ref.shape
    parts = lags_ref.shape[0]
    width = channels // parts
    block = length
    steps = channels // block
    peers = parts // steps
    copy = pltpu.make_async_copy
    loads = [
        copy(k_hbm, k_ref, sems.at[0]),
        copy(x_hbm, x_ref, sems.at[1]),
        copy(taps_hbm, taps_ref, sems.at[2]),
        copy(lags_hbm, lags_ref, sems.at[3]),
    ]
    for c in loads:
        c.start()

    src = iota((length, length), 0)
    dst = iota((length, length), 1)
    shifts = jnp.concatenate([one_hot(src == dst + i) for i in range(3)], axis=0)
    identity = one_hot(src == dst)
    hit = src == jnp.where(dst % 4 < 2, length - 2 + dst % 4, dst % 4 - 2)
    pick = jnp.concatenate([one_hot(hit & (dst % 8 < 4)), one_hot(hit & (dst % 8 >= 4))], axis=0)
    own = (dst // 8) == (src % width)
    tail = 8 * peers
    row = iota((tail, block), 0)
    gather = one_hot((row % 8 == 1) & (row // 8 == iota((tail, block), 1) // width))
    row = iota((tail, peers), 0)
    place = one_hot((row % 8 == 0) & (row // 8 == iota((tail, peers), 1)))

    for c in loads:
        c.wait()

    def short(moved, m, lanes):
        a, b, c = (taps_ref[m, i : i + 1, lanes] * moved[i * length : (i + 1) * length] for i in range(3))
        return a + b + c

    def gate(i):
        rows = slice(i * block, (i + 1) * block)
        k = k_ref[rows, :]
        x = x_ref[rows, :]
        edges = dot(jnp.concatenate([k, x], axis=1), pick)
        gated = short(dot_t(shifts, k), 1, rows) * short(dot_t(shifts, x), 2, rows)
        edges = jnp.where(own, edges, 0.0).astype(BF16)
        return jnp.where(src < 2, 0.0, gated).astype(BF16), edges

    def put(i, gated, edges):
        gated = dot_t(identity, gated).astype(BF16)
        rest = dot(gather, edges) + dot(place, lags_ref[i * peers : (i + 1) * peers, :])
        to = slice(i * peers, (i + 1) * peers)
        out_ref[to, 0:width, :] = gated.reshape(peers, width, length)
        out_ref[to, width : width + 8, :] = rest.astype(BF16).reshape(peers, 8, length)

    ahead = gate(0)
    for i in range(steps):
        current = ahead
        if i + 1 < steps:
            ahead = gate(i + 1)
        put(i, *current)
    store = copy(out_ref, out_hbm, sems.at[4])
    store.start()
    store.wait()


def conv_kernel(got_ref, weights_ref, skip_ref, out_ref):
    parts, _, length = got_ref.shape
    width = out_ref.shape[1]
    pairs = parts // 2
    at_stretch = places(ORDER_IN)

    tail = jnp.concatenate([got_ref[i, width : width + 8, :] for i in at_stretch], axis=0)
    row = iota((parts, 8 * parts), 0)
    col = iota((parts, 8 * parts), 1) - 1
    own = dot(one_hot(col == 8 * row), tail)
    last = dot(one_hot(col == 8 * row - 8), tail)
    lane = iota((parts, length), 1)
    joined = jnp.where(lane % 4 < 2, last, own)
    short = (
        weights_ref[0:1, :] * joined
        + weights_ref[1:2, :] * pltpu.roll(joined, 1, 1)
        + weights_ref[2:3, :] * pltpu.roll(joined, 2, 1)
    )
    first = short * pltpu.roll(short, length - 4, 1)
    lane = iota((width, length), 1)
    keep = (lane // 8 == iota((width, length), 0)) & (lane % 8 >= 2) & (lane % 8 < 4)
    src = iota((length, length), 0)
    dst = iota((length, length), 1)
    move = one_hot((src % 8 - 2 == dst) & (dst < 2))
    repeated = [jnp.where(keep, first[s : s + 1, :], 0.0).astype(BF16) for s in range(parts)]
    fixed = dot(jnp.concatenate(repeated, axis=0), move).astype(BF16)
    pieces = [got_ref[i, 0:width, :] + fixed[s * width : (s + 1) * width] for s, i in enumerate(at_stretch)]
    panel = jnp.concatenate(
        [jnp.concatenate(pieces[0::2], axis=0), jnp.concatenate(pieces[1::2], axis=0)], axis=1
    )

    upper = dst >= src

    def turn(b):
        taps = got_ref[at_stretch[b], width : width + 1, :].astype(F32)
        return pltpu.roll(jnp.broadcast_to(taps, (length, length)), 0, 1, stride=1, stride_axis=0)

    skip = jnp.concatenate([skip_ref[...]] * 2, axis=1)
    total = panel.astype(F32) * jnp.concatenate([skip] * pairs, axis=0)
    before = jnp.zeros((length, length), F32)
    left = jnp.zeros((length, length), BF16)
    for b in range(pairs):
        even, odd = turn(2 * b), turn(2 * b + 1)
        here = jnp.where(upper, even, before).astype(BF16)
        right = jnp.where(upper, odd, even).astype(BF16)
        block = jnp.concatenate(
            [jnp.concatenate([here, right], axis=1), jnp.concatenate([left, here], axis=1)], axis=0
        )
        before, left = odd, right
        live = (pairs - b) * width
        term = dot(panel[:live], block)
        if b:
            term = jnp.concatenate([jnp.zeros((b * width, 2 * length), F32), term], axis=0)
        total = total + term
    total = total.astype(BF16)
    for i, stretch in enumerate(ORDER_OUT):
        at = (stretch // 2) * width
        out_ref[i] = total[at : at + width, (stretch % 2) * length : (stretch % 2 + 1) * length]


def mix_kernel(back_ref, q_ref, out_ref):
    parts, width, length = back_ref.shape
    at_device = places(ORDER_OUT)
    for i, device in enumerate(ORDER_IN):
        rows = pl.ds(i * width, width)
        out_ref[rows, :] = (q_ref[rows, :] * back_ref[at_device[device]].astype(F32)).astype(BF16)


def call(kernel, out_shape, scratch=(), near=True):
    shape, dtype = out_shape
    out = pltpu.VMEM(shape, dtype) if near and not INTERPRET else jax.ShapeDtypeStruct(shape, dtype)
    return pl.pallas_call(
        kernel,
        out_shape=out,
        scratch_shapes=list(scratch),
        interpret=INTERPRET,
        name=kernel.__name__,
    )


def near(x):
    return x if INTERPRET else pltpu.with_memory_space_constraint(x, pltpu.VMEM)


def short_conv(stream, before, weights):
    joined = jnp.concatenate([before, stream], axis=1).astype(F32)
    length = stream.shape[1]
    return (
        weights[0][:, None] * joined[:, 2:]
        + weights[1][:, None] * joined[:, 1 : length + 1]
        + weights[2][:, None] * joined[:, 0:length]
    )


def exchange(chunks, order):
    return lax.all_to_all(
        chunks, "ctx", split_axis=0, concat_axis=0, tiled=True, axis_index_groups=[list(order)]
    )


def body(q_stream, k_stream, x_stream, short_taps, skip_gain, filter_taps):
    channels, length = q_stream.shape
    parts = lax.axis_size("ctx")
    width = channels // parts
    sent = pl.pallas_call(
        pack_kernel,
        out_shape=jax.ShapeDtypeStruct((parts, ROWS, length), BF16),
        in_specs=[pl.BlockSpec(memory_space=pl.ANY)] * 4,
        out_specs=pl.BlockSpec(memory_space=pl.ANY),
        scratch_shapes=[
            pltpu.VMEM((channels, length), BF16),
            pltpu.VMEM((channels, length), BF16),
            pltpu.VMEM(short_taps.shape, F32),
            pltpu.VMEM(filter_taps.shape, BF16),
            pltpu.VMEM((parts, ROWS, length), BF16),
            pltpu.SemaphoreType.DMA((5,)),
        ],
        interpret=INTERPRET,
        name="pack_kernel",
    )(k_stream, x_stream, short_taps, filter_taps)
    got = exchange(sent, ORDER_IN)

    pairs = [(i, i + 1) for i in range(parts - 1)]
    before = lax.ppermute(q_stream[:, -2:], "ctx", pairs)
    q_short = lax.optimization_barrier(short_conv(q_stream, before, short_taps[0]))
    first = jnp.asarray(places(ORDER_IN), jnp.int32)[lax.axis_index("ctx")] * width
    own = lax.dynamic_slice_in_dim(short_taps[1:], first, width, 2)
    own = jnp.repeat(jnp.transpose(own, (1, 2, 0)).reshape(3, 2 * width), 4, axis=1)
    weights = jnp.concatenate([own, jnp.zeros((5, length), F32)], axis=0)
    skip = lax.dynamic_slice_in_dim(skip_gain, first, width, 0)
    skip = jnp.broadcast_to(skip[:, None], (width, length))

    parted = call(
        conv_kernel,
        ((parts, width, length), BF16),
    )(near(got), near(weights), near(skip))
    back = exchange(parted, ORDER_OUT)
    return call(mix_kernel, ((channels, length), BF16), near=False)(near(back), near(q_short))


def solution(mesh):
    return jax.shard_map(
        body,
        mesh=mesh,
        in_specs=(
            P("ch", "ctx"),
            P("ch", "ctx"),
            P("ch", "ctx"),
            P(None, None, "ch"),
            P("ch"),
            P("ch", "ctx"),
        ),
        out_specs=P("ch", "ctx"),
        check_vma=False,
    )
```

```python
import jax
import jax.numpy as jnp
from jax import lax
from jax.experimental import pallas as pl
from jax.experimental.pallas import tpu as pltpu
from jax.sharding import PartitionSpec as P

INTERPRET = False
LANES = 128
EXTRA = 2
def ring_order(z0, x0, c0):
    return tuple(
        ((z + z0) % 4) * 8 + ((x + x0) % 4) * 2 + (c + c0) % 2
        for x in range(4)
        for z in range(4)
        for c in range(2)
    )


ORDER_IN = ring_order(2, 2, 1)
ORDER_OUT = ORDER_IN


def slot_of(i):
    return ((i // 2 + 2) % 4) * 8 + ((i // 8 + 2) % 4) * 2 + (i + 1) % 2


F32 = jnp.float32
BF16 = jnp.bfloat16


def iota(shape, dim):
    return lax.broadcasted_iota(jnp.int32, shape, dim)


def one_hot(mask):
    return jnp.where(mask, 1.0, 0.0).astype(BF16)


def places(order):
    return [order.index(i) for i in range(len(order))]


def dot(a, b):
    return jnp.dot(a, b, preferred_element_type=F32)


def dot_t(a, b):
    return lax.dot_general(a, b, (((1,), (1,)), ((), ())), preferred_element_type=F32)


def pack_kernel(
    k_hbm, x_hbm, taps_hbm, lags_hbm, gain_hbm, out_hbm, weights_ref, skip_ref,
    k_ref, x_ref, taps_ref, lags_ref, gain_ref, out_ref, sems,
):
    channels, length = k_ref.shape
    parts = lags_ref.shape[0]
    width = channels // parts
    block = length
    steps = channels // block
    peers = parts // steps
    copy = pltpu.make_async_copy
    pairs = [(k_hbm, k_ref), (x_hbm, x_ref), (taps_hbm, taps_ref), (lags_hbm, lags_ref), (gain_hbm, gain_ref)]
    loads = [copy(a, b, sems.at[i]) for i, (a, b) in enumerate(pairs)]
    for c in loads:
        c.start()

    src = iota((length, length), 0)
    dst = iota((length, length), 1)
    shifts = jnp.concatenate([one_hot(src == dst + i) for i in range(3)], axis=0)
    kind = (dst + 2) % 8
    hit = src == jnp.where(kind % 4 < 2, length - 2 + kind % 4, kind % 4 - 2)
    pick = jnp.concatenate([one_hot(hit & (kind < 4)), one_hot(hit & (kind >= 4))], axis=0)
    own = (dst + 2 + 8 * src) % length < 8
    stride = width + EXTRA
    row = iota((peers * stride, block), 0)
    col = iota((peers * stride, block), 1)
    place = one_hot((row // stride == col // width) & (row % stride == col % width))
    gather = one_hot((row // stride == col // width) & (row % stride == width + 1))
    row = iota((peers * stride, peers), 0)
    spare = one_hot(row == iota((peers * stride, peers), 1) * stride + width)

    for c in loads:
        c.wait()

    def short(moved, m, lanes):
        a, b, c = (taps_ref[m, i : i + 1, lanes] * moved[i * length : (i + 1) * length] for i in range(3))
        return a + b + c

    def gate(i):
        rows = slice(i * block, (i + 1) * block)
        k = k_ref[rows, :]
        x = x_ref[rows, :]
        edges = dot(jnp.concatenate([k, x], axis=1), pick)
        gated = short(dot_t(shifts, k), 1, rows) * short(dot_t(shifts, x), 2, rows)
        edges = jnp.where(own, edges, 0.0).astype(BF16)
        return jnp.where(src < 2, 0.0, gated).astype(BF16), edges

    def put(i, gated, edges):
        chunks = dot_t(place, gated) + dot(gather, edges) + dot(spare, lags_ref[i * peers : (i + 1) * peers, :])
        out_ref[i * peers * stride : (i + 1) * peers * stride, :] = chunks.astype(BF16)

    stores = []
    ahead = gate(0)
    for i in range(steps):
        current = ahead
        if i + 1 < steps:
            ahead = gate(i + 1)
        put(i, *current)
        to = pl.ds(i * peers * stride, peers * stride)
        stores.append(copy(out_ref.at[to], out_hbm.at[to], sems.at[5 + i]))
        stores[-1].start()

    rows = jnp.concatenate([taps_ref[1], taps_ref[2], gain_ref[...], jnp.zeros((1, channels), F32)], axis=0)
    rows = pltpu.roll(rows, (channels - slot_of(lax.axis_index("ctx")) * width) % channels, 1)[:, :length]
    columns = rows.T[:width]
    lane = iota((width, length), 1)
    mine = (lane + 2 + 8 * iota((width, length), 0)) % length < 8
    parted = []
    for j in range(3):
        both = jnp.where((lane + 2) % 8 < 4, columns[:, j : j + 1], columns[:, 3 + j : 4 + j])
        parted.append(jnp.sum(jnp.where(mine, both, 0.0), axis=0, keepdims=True))
    weights_ref[...] = jnp.concatenate(parted + [jnp.zeros((5, length), F32)], axis=0)
    skip_ref[...] = jnp.broadcast_to(columns[:, 6:7], (width, length))
    for c in stores:
        c.wait()


def conv_kernel(got_ref, weights_ref, skip_ref, out_ref):
    parts, width, length = out_ref.shape
    pairs = parts // 2
    stride = width + EXTRA
    at_stretch = places(ORDER_IN)

    lane = iota((parts, length), 1)
    at = [i * stride + width + 1 for i in at_stretch]
    own = jnp.concatenate([got_ref[i : i + 1, :].astype(F32) for i in at], axis=0)
    last = jnp.concatenate([jnp.zeros((1, length), F32), own[: parts - 1]], axis=0)
    joined = jnp.where((lane + 2) % 4 < 2, last, own)
    short = (
        weights_ref[0:1, :] * joined
        + weights_ref[1:2, :] * pltpu.roll(joined, 1, 1)
        + weights_ref[2:3, :] * pltpu.roll(joined, 2, 1)
    )
    first = short * pltpu.roll(short, length - 4, 1)
    src = iota((length, length), 0)
    dst = iota((length, length), 1)
    head = iota((width, length), 1) < 2

    def fixed(s):
        rows = jnp.broadcast_to(first[s : s + 1, :], (width, length))
        rows = pltpu.roll(rows, 0, 1, stride=8, stride_axis=0)
        return jnp.where(head, rows, got_ref[at_stretch[s] * stride : at_stretch[s] * stride + width, :].astype(F32))

    pieces = [fixed(s) for s in range(parts)]
    wide = jnp.concatenate(
        [jnp.concatenate(pieces[0::2], axis=0), jnp.concatenate(pieces[1::2], axis=0)], axis=1
    )
    panel = wide.astype(BF16)
    wide = panel.astype(F32)

    upper = dst >= src

    def turn(b):
        taps = got_ref[at_stretch[b] * stride + width : at_stretch[b] * stride + width + 1, :].astype(F32)
        return pltpu.roll(jnp.broadcast_to(taps, (length, length)), 0, 1, stride=1, stride_axis=0)

    skip = jnp.concatenate([skip_ref[...]] * 2, axis=1)
    total = wide * jnp.concatenate([skip] * pairs, axis=0)
    before = jnp.zeros((length, length), F32)
    left = jnp.zeros((length, length), BF16)
    for b in range(pairs):
        even, odd = turn(2 * b), turn(2 * b + 1)
        here = jnp.where(upper, even, before).astype(BF16)
        right = jnp.where(upper, odd, even).astype(BF16)
        block = jnp.concatenate(
            [jnp.concatenate([here, right], axis=1), jnp.concatenate([left, here], axis=1)], axis=0
        )
        before, left = odd, right
        live = (pairs - b) * width
        term = dot(panel[:live], block)
        if b:
            term = jnp.concatenate([jnp.zeros((b * width, 2 * length), F32), term], axis=0)
        total = total + term
    total = total.astype(BF16)
    for i, stretch in enumerate(ORDER_OUT):
        at = (stretch // 2) * width
        out_ref[i] = total[at : at + width, (stretch % 2) * length : (stretch % 2 + 1) * length]


def mix_kernel(back_ref, q_ref, out_ref):
    parts, width, length = back_ref.shape
    at_device = places(ORDER_OUT)
    for i, device in enumerate(ORDER_IN):
        rows = pl.ds(i * width, width)
        out_ref[rows, :] = (q_ref[rows, :] * back_ref[at_device[device]].astype(F32)).astype(BF16)


def call(kernel, out_shape, scratch=(), near=True):
    shape, dtype = out_shape
    out = pltpu.VMEM(shape, dtype) if near and not INTERPRET else jax.ShapeDtypeStruct(shape, dtype)
    return pl.pallas_call(
        kernel,
        out_shape=out,
        scratch_shapes=list(scratch),
        interpret=INTERPRET,
        name=kernel.__name__,
    )


def near(x):
    return x if INTERPRET else pltpu.with_memory_space_constraint(x, pltpu.VMEM)


def short_conv(stream, before, weights):
    joined = jnp.concatenate([before, stream], axis=1).astype(F32)
    length = stream.shape[1]
    return (
        weights[0][:, None] * joined[:, 2:]
        + weights[1][:, None] * joined[:, 1 : length + 1]
        + weights[2][:, None] * joined[:, 0:length]
    )


def exchange(chunks, order):
    return lax.all_to_all(
        chunks, "ctx", split_axis=0, concat_axis=0, tiled=True, axis_index_groups=[list(order)]
    )


def body(q_stream, k_stream, x_stream, short_taps, skip_gain, filter_taps):
    channels, length = q_stream.shape
    parts = lax.axis_size("ctx")
    width = channels // parts
    near_shape = jax.ShapeDtypeStruct if INTERPRET else pltpu.VMEM
    sent, weights, skip = pl.pallas_call(
        pack_kernel,
        out_shape=(
            jax.ShapeDtypeStruct((parts * (width + EXTRA), length), BF16),
            near_shape((8, length), F32),
            near_shape((width, length), F32),
        ),
        in_specs=[pl.BlockSpec(memory_space=pl.ANY)] * 5,
        out_specs=(
            pl.BlockSpec(memory_space=pl.ANY),
            pl.BlockSpec(memory_space=pltpu.VMEM),
            pl.BlockSpec(memory_space=pltpu.VMEM),
        ),
        scratch_shapes=[
            pltpu.VMEM((channels, length), BF16),
            pltpu.VMEM((channels, length), BF16),
            pltpu.VMEM(short_taps.shape, F32),
            pltpu.VMEM(filter_taps.shape, BF16),
            pltpu.VMEM((1, channels), F32),
            pltpu.VMEM((parts * (width + EXTRA), length), BF16),
            pltpu.SemaphoreType.DMA((5 + channels // length,)),
        ],
        interpret=INTERPRET,
        name="pack_kernel",
    )(k_stream, x_stream, short_taps, filter_taps, skip_gain[None, :])
    got = exchange(sent.reshape(parts, (width + EXTRA) // 2, 2, length), ORDER_IN).reshape(sent.shape)

    pairs = [(i, i + 1) for i in range(parts - 1)]
    before = lax.ppermute(q_stream[:, -2:], "ctx", pairs)
    q_short = lax.optimization_barrier(short_conv(q_stream, before, short_taps[0]))

    parted = call(
        conv_kernel,
        ((parts, width, length), BF16),
    )(near(got), near(weights), near(skip))
    back = exchange(parted, ORDER_OUT)
    return call(mix_kernel, ((channels, length), BF16), near=False)(near(back), near(q_short))


def solution(mesh):
    return jax.shard_map(
        body,
        mesh=mesh,
        in_specs=(
            P("ch", "ctx"),
            P("ch", "ctx"),
            P("ch", "ctx"),
            P(None, None, "ch"),
            P("ch"),
            P("ch", "ctx"),
        ),
        out_specs=P("ch", "ctx"),
        check_vma=False,
    )
```

```python
import jax
import jax.numpy as jnp
from jax import lax
from jax.experimental import pallas as pl
from jax.experimental.pallas import tpu as pltpu
from jax.sharding import PartitionSpec as P

INTERPRET = False
LANES = 128
FLUSH = 8
EXTRA = 2
def ring_order(z0, x0, c0):
    return tuple(
        ((z + z0) % 4) * 8 + ((x + x0) % 4) * 2 + (c + c0) % 2
        for x in range(4)
        for z in range(4)
        for c in range(2)
    )


ORDER_IN = ring_order(2, 2, 1)
ORDER_OUT = ORDER_IN


def slot_of(i):
    return ((i // 2 + 2) % 4) * 8 + ((i // 8 + 2) % 4) * 2 + (i + 1) % 2


F32 = jnp.float32
BF16 = jnp.bfloat16


def iota(shape, dim):
    return lax.broadcasted_iota(jnp.int32, shape, dim)


def one_hot(mask):
    return jnp.where(mask, 1.0, 0.0).astype(BF16)


def places(order):
    return [order.index(i) for i in range(len(order))]


def dot(a, b):
    return jnp.dot(a, b, preferred_element_type=F32)


def dot_t(a, b):
    return lax.dot_general(a, b, (((1,), (1,)), ((), ())), preferred_element_type=F32)


def pack_kernel(
    k_hbm, x_hbm, taps_hbm, lags_hbm, gain_hbm, out_hbm, weights_ref, skip_ref,
    k_ref, x_ref, taps_ref, lags_ref, gain_ref, out_ref, shifts, pick, own, place, gather, sems,
):
    channels, length = k_ref.shape
    parts = lags_ref.shape[0]
    width = channels // parts
    block = length
    steps = channels // block
    peers = parts // steps
    copy = pltpu.make_async_copy
    pairs = [(k_hbm, k_ref), (x_hbm, x_ref), (taps_hbm, taps_ref), (lags_hbm, lags_ref), (gain_hbm, gain_ref)]
    loads = [copy(a, b, sems.at[i]) for i, (a, b) in enumerate(pairs)]
    for c in loads:
        c.start()

    src = iota((length, length), 0)
    dst = iota((length, length), 1)
    for i in range(3):
        shifts[i * length : (i + 1) * length, :] = one_hot(src == dst + i)
    kind = (dst + 2) & 7
    hit = src == (((kind & 3) + length - 2) & (length - 1))
    pick[0:length, :] = one_hot(hit & (kind < 4))
    pick[length:, :] = one_hot(hit & (kind >= 4))
    own[...] = one_hot(((dst + 2 + 8 * src) & (length - 1)) < 8)
    stride = width + EXTRA
    row = iota((peers * stride, block), 0)
    col = iota((peers * stride, block), 1)
    peer = col // width
    place[...] = one_hot(row == col + EXTRA * peer)
    row = iota(gather.shape, 0)
    col = iota(gather.shape, 1)
    sample = (col < block) & (row == stride * (col // width) + width + 1)
    lag = (col >= block) & (col < block + peers) & (row == stride * (col - block) + width)
    gather[...] = one_hot(sample | lag)

    for c in loads:
        c.wait()

    def short(moved, m, i, at):
        lanes = slice(i * block, (i + 1) * block)
        a, b, c = (
            taps_ref[m, j : j + 1, lanes] * moved[j * length : (j + 1) * length, at * block : (at + 1) * block]
            for j in range(3)
        )
        return a + b + c

    def gate(i):
        rows = slice(i * block, (i + 2) * block)
        k = k_ref[rows, :]
        x = x_ref[rows, :]
        moved_k = dot_t(shifts[...], k)
        moved_x = dot_t(shifts[...], x)
        edges = dot(jnp.concatenate([k, x], axis=1), pick[...]).astype(BF16)
        gated = [short(moved_k, 1, i + j, j) * short(moved_x, 2, i + j, j) for j in range(2)]
        return jnp.concatenate(gated, axis=0).astype(BF16), edges

    def put(i, gated, edges):
        masked = jnp.concatenate([edges[:block] * own[...], edges[block:] * own[...]], axis=1)
        lags = lags_ref[i * peers : (i + 2) * peers, :].astype(F32)
        lags = jnp.concatenate([lags, jnp.concatenate([lags[peers:], lags[:peers]], axis=0)], axis=1)
        rest = jnp.concatenate([masked, lags.astype(BF16)], axis=0)
        chunks = (dot_t(place[...], gated) + dot(gather[...], rest)).astype(BF16)
        for j in range(2):
            at = (i + j) * peers * stride
            out_ref[at : at + peers * stride, :] = chunks[:, j * block : (j + 1) * block]

    stores = []
    ahead = gate(0)
    for i in range(0, steps, 2):
        current = ahead
        if i + 2 < steps:
            ahead = gate(i + 2)
        put(i, *current)
        to = pl.ds(i * peers * stride, 2 * peers * stride)
        stores.append(copy(out_ref.at[to], out_hbm.at[to], sems.at[5 + i]))
        stores[-1].start()

    rows = jnp.concatenate([taps_ref[1], taps_ref[2], gain_ref[...], jnp.zeros((1, channels), F32)], axis=0)
    rows = pltpu.roll(rows, (channels - slot_of(lax.axis_index("ctx")) * width) % channels, 1)[:, :length]
    columns = rows.T[:width]
    lane = iota((width, length), 1)
    mine = ((lane + 2 + 8 * iota((width, length), 0)) & (length - 1)) < 8
    parted = []
    for j in range(3):
        both = jnp.where(((lane + 2) & 7) < 4, columns[:, j : j + 1], columns[:, 3 + j : 4 + j])
        parted.append(jnp.sum(jnp.where(mine, both, 0.0), axis=0, keepdims=True))
    weights_ref[...] = jnp.concatenate(parted + [jnp.zeros((5, length), F32)], axis=0)
    skip_ref[...] = jnp.broadcast_to(columns[:, 6:7], (width, length))
    for c in stores:
        c.wait()


def conv_kernel(got_ref, weights_ref, skip_ref, out_hbm, out_ref, sem):
    parts, width, length = out_ref.shape
    pairs = parts // 2
    stride = width + EXTRA
    at_stretch = places(ORDER_IN)

    lane = iota((parts, length), 1)
    at = [i * stride + width + 1 for i in at_stretch]
    own = jnp.concatenate([got_ref[i : i + 1, :].astype(F32) for i in at], axis=0)
    last = jnp.concatenate([jnp.zeros((1, length), F32), own[: parts - 1]], axis=0)
    joined = jnp.where(((lane + 2) & 3) < 2, last, own)
    short = (
        weights_ref[0:1, :] * joined
        + weights_ref[1:2, :] * pltpu.roll(joined, 1, 1)
        + weights_ref[2:3, :] * pltpu.roll(joined, 2, 1)
    )
    first = short * pltpu.roll(short, length - 4, 1)
    src = iota((length, length), 0)
    dst = iota((length, length), 1)
    head = iota((width, length), 1) < 2

    def fixed(s):
        rows = jnp.broadcast_to(first[s : s + 1, :], (width, length))
        rows = pltpu.roll(rows, 0, 1, stride=8, stride_axis=0)
        return jnp.where(head, rows, got_ref[at_stretch[s] * stride : at_stretch[s] * stride + width, :].astype(F32))

    pieces = [fixed(s) for s in range(parts)]
    wide = jnp.concatenate(
        [jnp.concatenate(pieces[0::2], axis=0), jnp.concatenate(pieces[1::2], axis=0)], axis=1
    )
    panel = wide.astype(BF16)
    wide = panel.astype(F32)

    upper = dst >= src

    def turn(b):
        taps = got_ref[at_stretch[b] * stride + width : at_stretch[b] * stride + width + 1, :].astype(F32)
        return pltpu.roll(jnp.broadcast_to(taps, (length, length)), 0, 1, stride=1, stride_axis=0)

    skip = jnp.concatenate([skip_ref[...]] * 2, axis=1)
    total = wide * jnp.concatenate([skip] * pairs, axis=0)
    before = jnp.zeros((length, length), F32)
    left = jnp.zeros((length, length), BF16)
    for b in range(pairs):
        even, odd = turn(2 * b), turn(2 * b + 1)
        here = jnp.where(upper, even, before).astype(BF16)
        right = jnp.where(upper, odd, even).astype(BF16)
        block = jnp.concatenate(
            [jnp.concatenate([here, right], axis=1), jnp.concatenate([left, here], axis=1)], axis=0
        )
        before, left = odd, right
        live = (pairs - b) * width
        term = dot(panel[:live], block)
        if b:
            term = jnp.concatenate([jnp.zeros((b * width, 2 * length), F32), term], axis=0)
        total = total + term
        if b % FLUSH == FLUSH - 1:
            done = total[(b + 1 - FLUSH) * width : (b + 1) * width].astype(BF16)
            ready = []
            for i, stretch in enumerate(ORDER_OUT):
                at = stretch // 2 - (b + 1 - FLUSH)
                if 0 <= at < FLUSH:
                    lanes = slice((stretch % 2) * length, (stretch % 2 + 1) * length)
                    out_ref[i] = done[at * width : (at + 1) * width, lanes]
                    ready.append(i)
            starts = [i for i in ready if i - 1 not in ready]
            ends = [i + 1 for i in ready if i + 1 not in ready]
            for i, j in zip(starts, ends):
                pltpu.make_async_copy(out_ref.at[i:j], out_hbm.at[i:j], sem).start()
    pltpu.make_async_copy(out_ref, out_hbm, sem).wait()


def mix_kernel(back_ref, q_ref, out_ref):
    parts, width, length = back_ref.shape
    at_device = places(ORDER_OUT)
    for i, device in enumerate(ORDER_IN):
        rows = pl.ds(i * width, width)
        out_ref[rows, :] = (q_ref[rows, :] * back_ref[at_device[device]].astype(F32)).astype(BF16)


def call(kernel, out_shape, scratch=(), near=True):
    shape, dtype = out_shape
    out = pltpu.VMEM(shape, dtype) if near and not INTERPRET else jax.ShapeDtypeStruct(shape, dtype)
    return pl.pallas_call(
        kernel,
        out_shape=out,
        scratch_shapes=list(scratch),
        interpret=INTERPRET,
        name=kernel.__name__,
    )


def near(x):
    return x if INTERPRET else pltpu.with_memory_space_constraint(x, pltpu.VMEM)


def short_conv(stream, before, weights):
    joined = jnp.concatenate([before, stream], axis=1).astype(F32)
    length = stream.shape[1]
    return (
        weights[0][:, None] * joined[:, 2:]
        + weights[1][:, None] * joined[:, 1 : length + 1]
        + weights[2][:, None] * joined[:, 0:length]
    )


def exchange(chunks, order):
    return lax.all_to_all(
        chunks, "ctx", split_axis=0, concat_axis=0, tiled=True, axis_index_groups=[list(order)]
    )


def body(q_stream, k_stream, x_stream, short_taps, skip_gain, filter_taps):
    channels, length = q_stream.shape
    parts = lax.axis_size("ctx")
    width = channels // parts
    near_shape = jax.ShapeDtypeStruct if INTERPRET else pltpu.VMEM
    sent, weights, skip = pl.pallas_call(
        pack_kernel,
        out_shape=(
            jax.ShapeDtypeStruct((parts * (width + EXTRA), length), BF16),
            near_shape((8, length), F32),
            near_shape((width, length), F32),
        ),
        in_specs=[pl.BlockSpec(memory_space=pl.ANY)] * 5,
        out_specs=(
            pl.BlockSpec(memory_space=pl.ANY),
            pl.BlockSpec(memory_space=pltpu.VMEM),
            pl.BlockSpec(memory_space=pltpu.VMEM),
        ),
        scratch_shapes=[
            pltpu.VMEM((channels, length), BF16),
            pltpu.VMEM((channels, length), BF16),
            pltpu.VMEM(short_taps.shape, F32),
            pltpu.VMEM(filter_taps.shape, BF16),
            pltpu.VMEM((1, channels), F32),
            pltpu.VMEM((parts * (width + EXTRA), length), BF16),
            pltpu.VMEM((3 * length, length), BF16),
            pltpu.VMEM((2 * length, length), BF16),
            pltpu.VMEM((length, length), BF16),
            pltpu.VMEM((length // width * (width + EXTRA), length), BF16),
            pltpu.VMEM((length // width * (width + EXTRA), length + 2 * length // width), BF16),
            pltpu.SemaphoreType.DMA((5 + channels // length,)),
        ],
        interpret=INTERPRET,
        name="pack_kernel",
    )(k_stream, x_stream, short_taps, filter_taps, skip_gain[None, :])
    got = exchange(sent.reshape(parts, (width + EXTRA) // 2, 2, length), ORDER_IN).reshape(sent.shape)

    pairs = [(i, i + 1) for i in range(parts - 1)]
    before = lax.ppermute(q_stream[:, -2:], "ctx", pairs)
    q_short = lax.optimization_barrier(short_conv(q_stream, before, short_taps[0]))

    parted = pl.pallas_call(
        conv_kernel,
        out_shape=jax.ShapeDtypeStruct((parts, width, length), BF16),
        out_specs=pl.BlockSpec(memory_space=pl.ANY),
        scratch_shapes=[pltpu.VMEM((parts, width, length), BF16), pltpu.SemaphoreType.DMA],
        interpret=INTERPRET,
        name="conv_kernel",
    )(near(got), near(weights), near(skip))
    back = exchange(parted, ORDER_OUT)
    return call(mix_kernel, ((channels, length), BF16), near=False)(near(back), near(q_short))


def solution(mesh):
    return jax.shard_map(
        body,
        mesh=mesh,
        in_specs=(
            P("ch", "ctx"),
            P("ch", "ctx"),
            P("ch", "ctx"),
            P(None, None, "ch"),
            P("ch"),
            P("ch", "ctx"),
        ),
        out_specs=P("ch", "ctx"),
        check_vma=False,
    )
```

```python
import jax
import jax.numpy as jnp
from jax import lax
from jax.experimental import pallas as pl
from jax.experimental.pallas import tpu as pltpu
from jax.sharding import PartitionSpec as P

INTERPRET = False
LANES = 128
FLUSH = 8
EXTRA = 2
def ring_order(z0, x0, c0):
    return tuple(
        ((z + z0) % 4) * 8 + ((x + x0) % 4) * 2 + (c + c0) % 2
        for x in range(4)
        for z in range(4)
        for c in range(2)
    )


ORDER_IN = ring_order(2, 2, 1)
ORDER_OUT = ORDER_IN


def slot_of(i):
    return ((i // 2 + 2) % 4) * 8 + ((i // 8 + 2) % 4) * 2 + (i + 1) % 2


F32 = jnp.float32
BF16 = jnp.bfloat16


def iota(shape, dim):
    return lax.broadcasted_iota(jnp.int32, shape, dim)


def one_hot(mask):
    return jnp.where(mask, 1.0, 0.0).astype(BF16)


def places(order):
    return [order.index(i) for i in range(len(order))]


def dot(a, b):
    return jnp.dot(a, b, preferred_element_type=F32)


def dot_t(a, b):
    return lax.dot_general(a, b, (((1,), (1,)), ((), ())), preferred_element_type=F32)


def pack_kernel(
    k_hbm, x_hbm, taps_hbm, lags_hbm, gain_hbm, out_hbm, weights_ref, skip_ref,
    k_ref, x_ref, taps_ref, lags_ref, gain_ref, out_ref, shifts, pick, own, place, gather, sems,
):
    channels, length = k_ref.shape
    parts = lags_ref.shape[0]
    width = channels // parts
    block = length
    steps = channels // block
    peers = parts // steps
    copy = pltpu.make_async_copy
    pairs = [(k_hbm, k_ref), (x_hbm, x_ref), (taps_hbm, taps_ref), (lags_hbm, lags_ref), (gain_hbm, gain_ref)]
    loads = [copy(a, b, sems.at[i]) for i, (a, b) in enumerate(pairs)]
    for c in loads:
        c.start()

    src = iota((length, length), 0)
    dst = iota((length, length), 1)
    for i in range(3):
        shifts[i * length : (i + 1) * length, :] = one_hot(src == dst + i)
    kind = (dst + 2) & 7
    hit = src == (((kind & 3) + length - 2) & (length - 1))
    pick[0:length, :] = one_hot(hit & (kind < 4))
    pick[length:, :] = one_hot(hit & (kind >= 4))
    own[...] = one_hot(((dst + 2 + 8 * src) & (length - 1)) < 8)
    stride = width + EXTRA
    row = iota((peers * stride, block), 0)
    col = iota((peers * stride, block), 1)
    peer = col // width
    place[...] = one_hot(row == col + EXTRA * peer)
    row = iota(gather.shape, 0)
    col = iota(gather.shape, 1)
    sample = (col < block) & (row == stride * (col // width) + width + 1)
    lag = (col >= block) & (col < block + peers) & (row == stride * (col - block) + width)
    gather[...] = one_hot(sample | lag)

    for c in loads:
        c.wait()

    def short(moved, m, i, at):
        lanes = slice(i * block, (i + 1) * block)
        a, b, c = (
            taps_ref[m, j : j + 1, lanes] * moved[j * length : (j + 1) * length, at * block : (at + 1) * block]
            for j in range(3)
        )
        return a + b + c

    def gate(i):
        rows = slice(i * block, (i + 2) * block)
        k = k_ref[rows, :]
        x = x_ref[rows, :]
        moved_k = dot_t(shifts[...], k)
        moved_x = dot_t(shifts[...], x)
        edges = dot(jnp.concatenate([k, x], axis=1), pick[...]).astype(BF16)
        gated = [short(moved_k, 1, i + j, j) * short(moved_x, 2, i + j, j) for j in range(2)]
        return jnp.concatenate(gated, axis=0).astype(BF16), edges

    def put(i, gated, edges):
        masked = jnp.concatenate([edges[:block] * own[...], edges[block:] * own[...]], axis=1)
        lags = lags_ref[i * peers : (i + 2) * peers, :].astype(F32)
        lags = jnp.concatenate([lags, jnp.concatenate([lags[peers:], lags[:peers]], axis=0)], axis=1)
        rest = jnp.concatenate([masked, lags.astype(BF16)], axis=0)
        chunks = (dot_t(place[...], gated) + dot(gather[...], rest)).astype(BF16)
        for j in range(2):
            at = (i + j) * peers * stride
            out_ref[at : at + peers * stride, :] = chunks[:, j * block : (j + 1) * block]

    stores = []
    ahead = gate(0)
    for i in range(0, steps, 2):
        current = ahead
        if i + 2 < steps:
            ahead = gate(i + 2)
        put(i, *current)
        to = pl.ds(i * peers * stride, 2 * peers * stride)
        stores.append(copy(out_ref.at[to], out_hbm.at[to], sems.at[5 + i]))
        stores[-1].start()

    rows = jnp.concatenate([taps_ref[1], taps_ref[2], gain_ref[...], jnp.zeros((1, channels), F32)], axis=0)
    rows = pltpu.roll(rows, (channels - slot_of(lax.axis_index("ctx")) * width) % channels, 1)[:, :length]
    columns = rows.T[:width]
    lane = iota((width, length), 1)
    mine = ((lane + 2 + 8 * iota((width, length), 0)) & (length - 1)) < 8
    parted = []
    for j in range(3):
        both = jnp.where(((lane + 2) & 7) < 4, columns[:, j : j + 1], columns[:, 3 + j : 4 + j])
        parted.append(jnp.sum(jnp.where(mine, both, 0.0), axis=0, keepdims=True))
    weights_ref[...] = jnp.concatenate(parted + [jnp.zeros((5, length), F32)], axis=0)
    skip_ref[...] = jnp.broadcast_to(columns[:, 6:7], (width, length))
    for c in stores:
        c.wait()


def conv_kernel(got_ref, weights_ref, skip_ref, out_hbm, out_ref, sem):
    parts, width, length = out_ref.shape
    pairs = parts // 2
    stride = width + EXTRA
    at_stretch = places(ORDER_IN)

    lane = iota((parts, length), 1)
    at = [i * stride + width + 1 for i in at_stretch]
    own = jnp.concatenate([got_ref[i : i + 1, :].astype(F32) for i in at], axis=0)
    last = jnp.concatenate([jnp.zeros((1, length), F32), own[: parts - 1]], axis=0)
    joined = jnp.where(((lane + 2) & 3) < 2, last, own)
    short = (
        weights_ref[0:1, :] * joined
        + weights_ref[1:2, :] * pltpu.roll(joined, 1, 1)
        + weights_ref[2:3, :] * pltpu.roll(joined, 2, 1)
    )
    first = short * pltpu.roll(short, length - 4, 1)
    src = iota((length, length), 0)
    dst = iota((length, length), 1)
    head = iota((width, length), 1) < 2

    def fixed(s):
        rows = jnp.broadcast_to(first[s : s + 1, :], (width, length))
        rows = pltpu.roll(rows, 0, 1, stride=8, stride_axis=0)
        return jnp.where(head, rows, got_ref[at_stretch[s] * stride : at_stretch[s] * stride + width, :].astype(F32))

    pieces = [fixed(s) for s in range(parts)]
    wide = jnp.concatenate(
        [jnp.concatenate(pieces[0::2], axis=0), jnp.concatenate(pieces[1::2], axis=0)], axis=1
    )
    panel = wide.astype(BF16)
    wide = panel.astype(F32)

    upper = dst >= src

    def turn(b):
        taps = got_ref[at_stretch[b] * stride + width : at_stretch[b] * stride + width + 1, :].astype(F32)
        return pltpu.roll(jnp.broadcast_to(taps, (length, length)), 0, 1, stride=1, stride_axis=0)

    skip = jnp.concatenate([skip_ref[...]] * 2, axis=1)
    total = wide * jnp.concatenate([skip] * pairs, axis=0)
    before = jnp.zeros((length, length), F32)
    left = jnp.zeros((length, length), BF16)
    for b in range(pairs):
        even, odd = turn(2 * b), turn(2 * b + 1)
        here = jnp.where(upper, even, before).astype(BF16)
        right = jnp.where(upper, odd, even).astype(BF16)
        block = jnp.concatenate(
            [jnp.concatenate([here, right], axis=1), jnp.concatenate([left, here], axis=1)], axis=0
        )
        before, left = odd, right
        live = (pairs - b) * width
        term = dot(panel[:live], block)
        if b:
            term = jnp.concatenate([jnp.zeros((b * width, 2 * length), F32), term], axis=0)
        total = total + term
        if b % FLUSH == FLUSH - 1:
            done = total[(b + 1 - FLUSH) * width : (b + 1) * width].astype(BF16)
            ready = []
            for i, stretch in enumerate(ORDER_OUT):
                at = stretch // 2 - (b + 1 - FLUSH)
                if 0 <= at < FLUSH:
                    lanes = slice((stretch % 2) * length, (stretch % 2 + 1) * length)
                    out_ref[i] = done[at * width : (at + 1) * width, lanes]
                    ready.append(i)
            starts = [i for i in ready if i - 1 not in ready]
            ends = [i + 1 for i in ready if i + 1 not in ready]
            for i, j in zip(starts, ends):
                pltpu.make_async_copy(out_ref.at[i:j], out_hbm.at[i:j], sem).start()
    pltpu.make_async_copy(out_ref, out_hbm, sem).wait()


def mix_kernel(back_ref, q_ref, out_hbm, out_ref, sem):
    parts, width, length = back_ref.shape
    at_device = places(ORDER_OUT)
    for i, device in enumerate(ORDER_IN):
        rows = pl.ds(i * width, width)
        out_ref[rows, :] = (q_ref[rows, :] * back_ref[at_device[device]].astype(F32)).astype(BF16)
        if i % 8 == 7:
            rows = pl.ds((i - 7) * width, 8 * width)
            pltpu.make_async_copy(out_ref.at[rows], out_hbm.at[rows], sem).start()
    pltpu.make_async_copy(out_ref, out_hbm, sem).wait()


def call(kernel, out_shape, scratch=(), near=True):
    shape, dtype = out_shape
    out = pltpu.VMEM(shape, dtype) if near and not INTERPRET else jax.ShapeDtypeStruct(shape, dtype)
    return pl.pallas_call(
        kernel,
        out_shape=out,
        scratch_shapes=list(scratch),
        interpret=INTERPRET,
        name=kernel.__name__,
    )


def near(x):
    return x if INTERPRET else pltpu.with_memory_space_constraint(x, pltpu.VMEM)


def short_conv(stream, before, weights):
    joined = jnp.concatenate([before, stream], axis=1).astype(F32)
    length = stream.shape[1]
    return (
        weights[0][:, None] * joined[:, 2:]
        + weights[1][:, None] * joined[:, 1 : length + 1]
        + weights[2][:, None] * joined[:, 0:length]
    )


def exchange(chunks, order):
    return lax.all_to_all(
        chunks, "ctx", split_axis=0, concat_axis=0, tiled=True, axis_index_groups=[list(order)]
    )


def body(q_stream, k_stream, x_stream, short_taps, skip_gain, filter_taps):
    channels, length = q_stream.shape
    parts = lax.axis_size("ctx")
    width = channels // parts
    near_shape = jax.ShapeDtypeStruct if INTERPRET else pltpu.VMEM
    sent, weights, skip = pl.pallas_call(
        pack_kernel,
        out_shape=(
            jax.ShapeDtypeStruct((parts * (width + EXTRA), length), BF16),
            near_shape((8, length), F32),
            near_shape((width, length), F32),
        ),
        in_specs=[pl.BlockSpec(memory_space=pl.ANY)] * 5,
        out_specs=(
            pl.BlockSpec(memory_space=pl.ANY),
            pl.BlockSpec(memory_space=pltpu.VMEM),
            pl.BlockSpec(memory_space=pltpu.VMEM),
        ),
        scratch_shapes=[
            pltpu.VMEM((channels, length), BF16),
            pltpu.VMEM((channels, length), BF16),
            pltpu.VMEM(short_taps.shape, F32),
            pltpu.VMEM(filter_taps.shape, BF16),
            pltpu.VMEM((1, channels), F32),
            pltpu.VMEM((parts * (width + EXTRA), length), BF16),
            pltpu.VMEM((3 * length, length), BF16),
            pltpu.VMEM((2 * length, length), BF16),
            pltpu.VMEM((length, length), BF16),
            pltpu.VMEM((length // width * (width + EXTRA), length), BF16),
            pltpu.VMEM((length // width * (width + EXTRA), length + 2 * length // width), BF16),
            pltpu.SemaphoreType.DMA((5 + channels // length,)),
        ],
        interpret=INTERPRET,
        name="pack_kernel",
        compiler_params=pltpu.CompilerParams(),
    )(k_stream, x_stream, short_taps, filter_taps, skip_gain[None, :])
    got = exchange(sent.reshape(parts, (width + EXTRA) // 2, 2, length), ORDER_IN).reshape(sent.shape)

    pairs = [(i, i + 1) for i in range(parts - 1)]
    before = lax.ppermute(q_stream[:, -2:], "ctx", pairs)
    q_short = lax.optimization_barrier(short_conv(q_stream, before, short_taps[0]))

    parted = pl.pallas_call(
        conv_kernel,
        out_shape=jax.ShapeDtypeStruct((parts, width, length), BF16),
        out_specs=pl.BlockSpec(memory_space=pl.ANY),
        scratch_shapes=[pltpu.VMEM((parts, width, length), BF16), pltpu.SemaphoreType.DMA],
        interpret=INTERPRET,
        name="conv_kernel",
    )(near(got), near(weights), near(skip))
    back = exchange(parted, ORDER_OUT)
    return pl.pallas_call(
        mix_kernel,
        out_shape=jax.ShapeDtypeStruct((channels, length), BF16),
        out_specs=pl.BlockSpec(memory_space=pl.ANY),
        scratch_shapes=[pltpu.VMEM((channels, length), BF16), pltpu.SemaphoreType.DMA],
        interpret=INTERPRET,
        name="mix_kernel",
    )(near(back), near(q_short))


def solution(mesh):
    return jax.shard_map(
        body,
        mesh=mesh,
        in_specs=(
            P("ch", "ctx"),
            P("ch", "ctx"),
            P("ch", "ctx"),
            P(None, None, "ch"),
            P("ch"),
            P("ch", "ctx"),
        ),
        out_specs=P("ch", "ctx"),
        check_vma=False,
    )
```

```python
import jax
import jax.numpy as jnp
from jax import lax
from jax.experimental import pallas as pl
from jax.experimental.pallas import tpu as pltpu
from jax.sharding import PartitionSpec as P

INTERPRET = False
LANES = 128
FLUSH = 8
EXTRA = 2
def ring_order(z0, x0, c0):
    return tuple(
        ((z + z0) % 4) * 8 + ((x + x0) % 4) * 2 + (c + c0) % 2
        for x in range(4)
        for z in range(4)
        for c in range(2)
    )


ORDER_IN = ring_order(2, 2, 1)
ORDER_OUT = ORDER_IN


def slot_of(i):
    return ((i // 2 + 2) % 4) * 8 + ((i // 8 + 2) % 4) * 2 + (i + 1) % 2


F32 = jnp.float32
BF16 = jnp.bfloat16


def iota(shape, dim):
    return lax.broadcasted_iota(jnp.int32, shape, dim)


def one_hot(mask):
    return jnp.where(mask, 1.0, 0.0).astype(BF16)


def places(order):
    return [order.index(i) for i in range(len(order))]


def dot(a, b):
    return jnp.dot(a, b, preferred_element_type=F32)


def dot_t(a, b):
    return lax.dot_general(a, b, (((1,), (1,)), ((), ())), preferred_element_type=F32)


def pack_kernel(
    k_hbm, x_hbm, taps_hbm, lags_hbm, gain_hbm, out_hbm, weights_ref, skip_ref,
    k_ref, x_ref, taps_ref, lags_ref, gain_ref, out_ref, shifts, pick, own, place, gather, sems,
):
    channels, length = k_ref.shape
    parts = lags_ref.shape[0]
    width = channels // parts
    block = length
    steps = channels // block
    peers = parts // steps
    copy = pltpu.make_async_copy
    pairs = [(k_hbm, k_ref), (x_hbm, x_ref), (taps_hbm, taps_ref), (lags_hbm, lags_ref), (gain_hbm, gain_ref)]
    loads = [copy(a, b, sems.at[i]) for i, (a, b) in enumerate(pairs)]
    for c in loads:
        c.start()

    src = iota((length, length), 0)
    dst = iota((length, length), 1)
    for i in range(3):
        shifts[i * length : (i + 1) * length, :] = one_hot(src == dst + i)
    kind = (dst + 2) & 7
    hit = src == (((kind & 3) + length - 2) & (length - 1))
    pick[0:length, :] = one_hot(hit & (kind < 4))
    pick[length:, :] = one_hot(hit & (kind >= 4))
    own[...] = one_hot(((dst + 2 + 8 * src) & (length - 1)) < 8)
    stride = width + EXTRA
    row = iota((peers * stride, block), 0)
    col = iota((peers * stride, block), 1)
    peer = col // width
    place[...] = one_hot(row == col + EXTRA * peer)
    row = iota(gather.shape, 0)
    col = iota(gather.shape, 1)
    sample = (col < block) & (row == stride * (col // width) + width + 1)
    lag = (col >= block) & (col < block + peers) & (row == stride * (col - block) + width)
    gather[...] = one_hot(sample | lag)

    for c in loads[:1] + loads[2:]:
        c.wait()

    def short(moved, m, i, at):
        lanes = slice(i * block, (i + 1) * block)
        a, b, c = (
            taps_ref[m, j : j + 1, lanes] * moved[j * length : (j + 1) * length, at * block : (at + 1) * block]
            for j in range(3)
        )
        return a + b + c

    def gate(i):
        rows = slice(i * block, (i + 2) * block)
        k = k_ref[rows, :]
        moved_k = dot_t(shifts[...], k)
        if i == 0:
            loads[1].wait()
        x = x_ref[rows, :]
        moved_x = dot_t(shifts[...], x)
        edges = dot(jnp.concatenate([k, x], axis=1), pick[...]).astype(BF16)
        gated = [short(moved_k, 1, i + j, j) * short(moved_x, 2, i + j, j) for j in range(2)]
        return jnp.concatenate(gated, axis=0).astype(BF16), edges

    def put(i, gated, edges):
        masked = jnp.concatenate([edges[:block] * own[...], edges[block:] * own[...]], axis=1)
        lags = lags_ref[i * peers : (i + 2) * peers, :].astype(F32)
        lags = jnp.concatenate([lags, jnp.concatenate([lags[peers:], lags[:peers]], axis=0)], axis=1)
        rest = jnp.concatenate([masked, lags.astype(BF16)], axis=0)
        chunks = (dot_t(place[...], gated) + dot(gather[...], rest)).astype(BF16)
        for j in range(2):
            at = (i + j) * peers * stride
            out_ref[at : at + peers * stride, :] = chunks[:, j * block : (j + 1) * block]

    stores = []
    ahead = gate(0)
    for i in range(0, steps, 2):
        current = ahead
        if i + 2 < steps:
            ahead = gate(i + 2)
        put(i, *current)
        to = pl.ds(i * peers * stride, 2 * peers * stride)
        stores.append(copy(out_ref.at[to], out_hbm.at[to], sems.at[5 + i]))
        stores[-1].start()

    rows = jnp.concatenate([taps_ref[1], taps_ref[2], gain_ref[...], jnp.zeros((1, channels), F32)], axis=0)
    rows = pltpu.roll(rows, (channels - slot_of(lax.axis_index("ctx")) * width) % channels, 1)[:, :length]
    columns = rows.T[:width]
    lane = iota((width, length), 1)
    mine = ((lane + 2 + 8 * iota((width, length), 0)) & (length - 1)) < 8
    parted = []
    for j in range(3):
        both = jnp.where(((lane + 2) & 7) < 4, columns[:, j : j + 1], columns[:, 3 + j : 4 + j])
        parted.append(jnp.sum(jnp.where(mine, both, 0.0), axis=0, keepdims=True))
    weights_ref[...] = jnp.concatenate(parted + [jnp.zeros((5, length), F32)], axis=0)
    skip_ref[...] = jnp.broadcast_to(columns[:, 6:7], (width, length))
    for c in stores:
        c.wait()


def conv_kernel(got_ref, weights_ref, skip_ref, out_hbm, out_ref, sem):
    parts, width, length = out_ref.shape
    pairs = parts // 2
    stride = width + EXTRA
    at_stretch = places(ORDER_IN)

    lane = iota((parts, length), 1)
    at = [i * stride + width + 1 for i in at_stretch]
    own = jnp.concatenate([got_ref[i : i + 1, :].astype(F32) for i in at], axis=0)
    last = jnp.concatenate([jnp.zeros((1, length), F32), own[: parts - 1]], axis=0)
    joined = jnp.where(((lane + 2) & 3) < 2, last, own)
    short = (
        weights_ref[0:1, :] * joined
        + weights_ref[1:2, :] * pltpu.roll(joined, 1, 1)
        + weights_ref[2:3, :] * pltpu.roll(joined, 2, 1)
    )
    first = short * pltpu.roll(short, length - 4, 1)
    src = iota((length, length), 0)
    dst = iota((length, length), 1)
    head = iota((width, length), 1) < 2

    def fixed(s):
        rows = jnp.broadcast_to(first[s : s + 1, :], (width, length))
        rows = pltpu.roll(rows, 0, 1, stride=8, stride_axis=0)
        return jnp.where(head, rows, got_ref[at_stretch[s] * stride : at_stretch[s] * stride + width, :].astype(F32))

    pieces = [fixed(s) for s in range(parts)]
    wide = jnp.concatenate(
        [jnp.concatenate(pieces[0::2], axis=0), jnp.concatenate(pieces[1::2], axis=0)], axis=1
    )
    panel = wide.astype(BF16)
    wide = panel.astype(F32)

    upper = dst >= src

    def turn(b):
        taps = got_ref[at_stretch[b] * stride + width : at_stretch[b] * stride + width + 1, :].astype(F32)
        return pltpu.roll(jnp.broadcast_to(taps, (length, length)), 0, 1, stride=1, stride_axis=0)

    skip = jnp.concatenate([skip_ref[...]] * 2, axis=1)
    total = wide * jnp.concatenate([skip] * pairs, axis=0)
    before = jnp.zeros((length, length), F32)
    left = jnp.zeros((length, length), BF16)
    for b in range(pairs):
        even, odd = turn(2 * b), turn(2 * b + 1)
        here = jnp.where(upper, even, before).astype(BF16)
        right = jnp.where(upper, odd, even).astype(BF16)
        block = jnp.concatenate(
            [jnp.concatenate([here, right], axis=1), jnp.concatenate([left, here], axis=1)], axis=0
        )
        before, left = odd, right
        live = (pairs - b) * width
        term = dot(panel[:live], block)
        if b:
            term = jnp.concatenate([jnp.zeros((b * width, 2 * length), F32), term], axis=0)
        total = total + term
        if b % FLUSH == FLUSH - 1:
            done = total[(b + 1 - FLUSH) * width : (b + 1) * width].astype(BF16)
            ready = []
            for i, stretch in enumerate(ORDER_OUT):
                at = stretch // 2 - (b + 1 - FLUSH)
                if 0 <= at < FLUSH:
                    lanes = slice((stretch % 2) * length, (stretch % 2 + 1) * length)
                    out_ref[i] = done[at * width : (at + 1) * width, lanes]
                    ready.append(i)
            starts = [i for i in ready if i - 1 not in ready]
            ends = [i + 1 for i in ready if i + 1 not in ready]
            for i, j in zip(starts, ends):
                pltpu.make_async_copy(out_ref.at[i:j], out_hbm.at[i:j], sem).start()
    pltpu.make_async_copy(out_ref, out_hbm, sem).wait()


def mix_kernel(back_ref, q_ref, out_ref):
    parts, width, length = back_ref.shape
    at_device = places(ORDER_OUT)
    for i, device in enumerate(ORDER_IN):
        rows = pl.ds(i * width, width)
        out_ref[rows, :] = (q_ref[rows, :] * back_ref[at_device[device]].astype(F32)).astype(BF16)


def call(kernel, out_shape, scratch=(), near=True):
    shape, dtype = out_shape
    out = pltpu.VMEM(shape, dtype) if near and not INTERPRET else jax.ShapeDtypeStruct(shape, dtype)
    return pl.pallas_call(
        kernel,
        out_shape=out,
        scratch_shapes=list(scratch),
        interpret=INTERPRET,
        name=kernel.__name__,
    )


def near(x):
    return x if INTERPRET else pltpu.with_memory_space_constraint(x, pltpu.VMEM)


def short_conv(stream, before, weights):
    joined = jnp.concatenate([before, stream], axis=1).astype(F32)
    length = stream.shape[1]
    return (
        weights[0][:, None] * joined[:, 2:]
        + weights[1][:, None] * joined[:, 1 : length + 1]
        + weights[2][:, None] * joined[:, 0:length]
    )


def exchange(chunks, order):
    return lax.all_to_all(
        chunks, "ctx", split_axis=0, concat_axis=0, tiled=True, axis_index_groups=[list(order)]
    )


def body(q_stream, k_stream, x_stream, short_taps, skip_gain, filter_taps):
    channels, length = q_stream.shape
    parts = lax.axis_size("ctx")
    width = channels // parts
    near_shape = jax.ShapeDtypeStruct if INTERPRET else pltpu.VMEM
    sent, weights, skip = pl.pallas_call(
        pack_kernel,
        out_shape=(
            jax.ShapeDtypeStruct((parts * (width + EXTRA), length), BF16),
            near_shape((8, length), F32),
            near_shape((width, length), F32),
        ),
        in_specs=[pl.BlockSpec(memory_space=pl.ANY)] * 5,
        out_specs=(
            pl.BlockSpec(memory_space=pl.ANY),
            pl.BlockSpec(memory_space=pltpu.VMEM),
            pl.BlockSpec(memory_space=pltpu.VMEM),
        ),
        scratch_shapes=[
            pltpu.VMEM((channels, length), BF16),
            pltpu.VMEM((channels, length), BF16),
            pltpu.VMEM(short_taps.shape, F32),
            pltpu.VMEM(filter_taps.shape, BF16),
            pltpu.VMEM((1, channels), F32),
            pltpu.VMEM((parts * (width + EXTRA), length), BF16),
            pltpu.VMEM((3 * length, length), BF16),
            pltpu.VMEM((2 * length, length), BF16),
            pltpu.VMEM((length, length), BF16),
            pltpu.VMEM((length // width * (width + EXTRA), length), BF16),
            pltpu.VMEM((length // width * (width + EXTRA), length + 2 * length // width), BF16),
            pltpu.SemaphoreType.DMA((5 + channels // length,)),
        ],
        interpret=INTERPRET,
        name="pack_kernel",
    )(k_stream, x_stream, short_taps, filter_taps, skip_gain[None, :])
    got = exchange(sent.reshape(parts, (width + EXTRA) // 2, 2, length), ORDER_IN).reshape(sent.shape)

    pairs = [(i, i + 1) for i in range(parts - 1)]
    before = lax.ppermute(q_stream[:, -2:], "ctx", pairs)
    q_short = lax.optimization_barrier(short_conv(q_stream, before, short_taps[0]))

    parted = pl.pallas_call(
        conv_kernel,
        out_shape=jax.ShapeDtypeStruct((parts, width, length), BF16),
        out_specs=pl.BlockSpec(memory_space=pl.ANY),
        scratch_shapes=[pltpu.VMEM((parts, width, length), BF16), pltpu.SemaphoreType.DMA],
        interpret=INTERPRET,
        name="conv_kernel",
    )(near(got), near(weights), near(skip))
    back = exchange(parted, ORDER_OUT)
    return call(mix_kernel, ((channels, length), BF16), near=False)(near(back), near(q_short))


def solution(mesh):
    return jax.shard_map(
        body,
        mesh=mesh,
        in_specs=(
            P("ch", "ctx"),
            P("ch", "ctx"),
            P("ch", "ctx"),
            P(None, None, "ch"),
            P("ch"),
            P("ch", "ctx"),
        ),
        out_specs=P("ch", "ctx"),
        check_vma=False,
    )
```
